128 devices in a mesh: pix: 8 (over x, z_lo), act: 16 (over z_hi, y, core).
Axes of the slice: x: 4, y: 4, z: 4 (z_hi: 2, z_lo: 2; z = z_hi * 2 + z_lo), core: 2. Of those that a mesh axis runs over, the one named last changes fastest.
Arguments:
- jacobian: bfloat16 [2048, 18432], P('pix', 'act'), may hold values from -0.125 to 0.125
- dark_field: float32 [2048], P('pix'), may hold values from -6 to 6
- update: float32 [18432], P('act'), may hold values from -3 to 3
- pixel_mask: int32 [2048], P('pix'), may hold values 0 or 1
- act_mask: int32 [18432], P('act'), may hold values 0 or 1
Outputs:
- gram_matrix: float32 [18432, 18432], P('act', 'pix')
- projected: float32 [18432], P('act')
- predicted: float32 [2048], P('pix')
The draws below stay inside these ranges and needn't reach their ends.
All inputs are finite; a program needn't handle non-finite values. No bound on the sum of `pixel_mask` or of `act_mask` on one device may be relied on, other than what follows from the above.
Results may differ from the reference program's by a relative error of at most 0.0003.
Values may be sent and summed in bfloat16 or wider, within the bound.
No kernel may reach another device: no remote copies, remote signals or barrier semaphores. Data moves between devices by JAX's collectives and lax.ppermute only.
A program may use at most 128 MiB of HBM per device.

```python
import jax
import jax.numpy as jnp
from jax import lax

NACT = 18432
ROWS = 2048


def plant(entries, key, smallest, largest):
    spot = [jax.random.randint(jax.random.fold_in(key, axis), (), 0, length) for axis, length in enumerate(entries.shape)]
    longest = entries.shape.index(max(entries.shape))
    neighbour = spot[:longest] + [(spot[longest] + 1) % entries.shape[longest]] + spot[longest + 1:]
    return entries.at[tuple(spot)].set(smallest).at[tuple(neighbour)].set(largest)


def block_levels(rng, dims, split, low, high):
    def one(dim, shards_of):
        draws = jax.random.uniform(jax.random.fold_in(jax.random.fold_in(rng, 6), dim), (shards_of,), jnp.float32, low / len(split), high / len(split))
        return jnp.repeat(jnp.exp(draws), dims[dim] // shards_of).reshape((-1,) + (1,) * (len(dims) - dim - 1))

    factor_of = one(*split[0])
    for cut in split[1:]:
        factor_of = factor_of * one(*cut)
    return factor_of


def noise(own_key, extent, width, most, pieces=(), held_as=jnp.bfloat16):
    drawn = width * jax.random.normal(own_key, extent, jnp.float32)
    if pieces:
        drawn = drawn * block_levels(own_key, extent, pieces, -0.22, 0.18)
    return jnp.clip(drawn, -most, most).astype(held_as)


def setup_inputs(seed: int = 0) -> dict:
    key_list = jax.random.split(jax.random.key(seed), 6)
    return {
        "jacobian": noise(key_list[0], (ROWS, NACT), ROWS ** -0.5, 0.125, ((0, 8), (1, 16))),
        "dark_field": noise(key_list[1], (ROWS,), 1.0, 6.0, ((0, 8),), jnp.float32),
        "update": noise(key_list[2], (NACT,), 0.5, 3.0, ((0, 16),), jnp.float32),
        "pixel_mask": plant((jax.random.randint(key_list[3], (ROWS,), 0, 4) < 3).astype(jnp.int32), jax.random.fold_in(key_list[3], 1), 0, 1),
        "act_mask": plant((jax.random.randint(key_list[4], (NACT,), 0, 8) < 7).astype(jnp.int32), jax.random.fold_in(key_list[4], 1), 0, 1),
    }


def reference(jacobian, dark_field, update, pixel_mask, act_mask):
    keep = (pixel_mask[:, None] * act_mask[None, :]) > 0
    masked_jac = jnp.where(keep, jacobian, jnp.zeros_like(jacobian))
    gram_matrix = lax.dot_general(masked_jac, masked_jac, (((0,), (0,)), ((), ())), preferred_element_type=jnp.float32)
    weighted = pixel_mask.astype(jnp.float32) * dark_field
    projected = jnp.dot(weighted, masked_jac.astype(jnp.float32), precision=lax.Precision.HIGHEST, preferred_element_type=jnp.float32)
    strokes = act_mask.astype(jnp.float32) * update
    predicted = jnp.dot(masked_jac.astype(jnp.float32), strokes, precision=lax.Precision.HIGHEST, preferred_element_type=jnp.float32)
    return gram_matrix, projected, predicted
```

```python
import functools

import jax
import jax.numpy as jnp
from jax import lax
from jax.experimental import pallas as pl
from jax.experimental.pallas import tpu as pltpu
from jax.sharding import PartitionSpec as P

F32 = jnp.float32
AXES = ("pix", "act")


def coords(device):
    pix, act = divmod(device, 16)
    return pix >> 1, (act >> 1) & 3, (act >> 3) * 2 + (pix & 1), act & 1


def device_of(x, y, z, core):
    return ((x % 4) * 2 + (z & 1)) * 16 + ((z >> 1) & 1) * 8 + (y % 4) * 2 + core


def send(value, route):
    pairs = [(device, device_of(*route(*coords(device)))) for device in range(128)]
    return lax.ppermute(value, AXES, pairs)


def transposed(x, y, z, core):
    return 2 * (z >> 1) + (y >> 1), x, 2 * (z & 1) + (y & 1), core


def along_x(step):
    return lambda x, y, z, core: (x + step, y, z, core)


def along_y(step):
    return lambda x, y, z, core: (x, y + step, z, core)


def z_pair(x, y, z, core):
    return x, y, z ^ 1, core


def z_half(x, y, z, core):
    return x, y, z ^ 2, core


def sibling(x, y, z, core):
    return x, y, z, core ^ 1


def gram(own, mine, theirs, rows, cols, tile):
    count = len(own)
    depth = rows * count

    def kernel(*refs):
        own_refs, mine_refs, their_refs = refs[:count], refs[count:2 * count], refs[2 * count:3 * count]
        out_ref, left, right, sems = refs[3 * count:]
        step = pl.program_id(0)
        pix, act = lax.axis_index("pix"), lax.axis_index("act")
        x, z_lo = pix // 2, pix % 2
        core, y, z_hi = act % 2, (act // 2) % 4, act // 8

        def copies():
            for slot in range(count):
                shift, flip = slot % 4, slot // 4
                own_block = ((x + 4 - shift) % 4) * 2 + (z_lo + flip) % 2
                part_block = ((y + 4 - shift) % 4) * 2 + (z_hi + flip) % 2
                own_rows = pl.ds(pl.multiple_of(own_block * rows, rows), rows)
                part_rows = pl.ds(pl.multiple_of(part_block * rows, rows), rows)
                here = pl.ds(pl.multiple_of(core * cols, cols), cols)
                there = pl.ds(pl.multiple_of((1 - core) * cols, cols), cols)
                yield pltpu.make_async_copy(own_refs[slot], left.at[own_rows, :], sems.at[0, slot])
                yield pltpu.make_async_copy(mine_refs[slot], right.at[part_rows, here], sems.at[1, slot])
                yield pltpu.make_async_copy(their_refs[slot], right.at[part_rows, there], sems.at[2, slot])

        @pl.when(step == 0)
        def _():
            for copy in copies():
                copy.start()
            for copy in copies():
                copy.wait()

        window = pl.ds(pl.multiple_of(step * tile, tile), tile)
        out_ref[...] = lax.dot_general(
            left[...], right[:, window], (((0,), (0,)), ((), ())), preferred_element_type=F32
        )

    return pl.pallas_call(
        kernel,
        grid=(2 * cols // tile,),
        in_specs=[pl.BlockSpec(memory_space=pl.ANY)] * (3 * count),
        out_specs=pl.BlockSpec((cols, tile), lambda step: (0, step)),
        out_shape=jax.ShapeDtypeStruct((cols, 2 * cols), F32),
        scratch_shapes=[
            pltpu.VMEM((depth, cols), jnp.bfloat16),
            pltpu.VMEM((depth, 2 * cols), jnp.bfloat16),
            pltpu.SemaphoreType.DMA((3, count)),
        ],
        compiler_params=pltpu.CompilerParams(vmem_limit_bytes=48 << 20),
        cost_estimate=pl.CostEstimate(
            flops=4 * depth * cols * cols, bytes_accessed=6 * depth * cols + 8 * cols * cols, transcendentals=0
        ),
        name="gram",
    )(*own, *mine, *theirs)


def local(jacobian, dark_field, update, pixel_mask, act_mask):
    rows, cols = jacobian.shape
    keep = pixel_mask[:, None] * act_mask[None, :] > 0
    masked_jac = jnp.where(keep, jacobian, jnp.zeros_like(jacobian))
    part = send(masked_jac, transposed)
    pair = send(masked_jac, z_pair)
    own = [masked_jac] + [send(masked_jac, along_x(s)) for s in (1, 2, 3)]
    own += [pair] + [send(pair, along_x(s)) for s in (1, 2, 3)]
    half = send(part, z_half)
    mine = [part] + [send(part, along_y(s)) for s in (1, 2, 3)]
    mine += [half] + [send(half, along_y(s)) for s in (1, 2, 3)]
    theirs = [send(piece, sibling) for piece in mine]
    gram_matrix = gram(own, mine, theirs, rows, cols, 256)

    weighted = pixel_mask.astype(F32) * dark_field
    strokes = act_mask.astype(F32) * update
    wide = masked_jac.astype(F32)
    projected = jnp.sum(wide * weighted[:, None], axis=0)
    predicted = jnp.sum(wide * strokes[None, :], axis=1)
    for route in (z_pair, along_x(2), along_x(1)):
        projected = projected + send(projected, route)
    for route in (sibling, z_half, along_y(2), along_y(1)):
        predicted = predicted + send(predicted, route)
    return (gram_matrix, projected, predicted)


def solution(mesh):
    return jax.shard_map(
        local,
        mesh=mesh,
        in_specs=(P("pix", "act"), P("pix"), P("act"), P("pix"), P("act")),
        out_specs=(P("act", "pix"), P("act"), P("pix")),
        check_vma=False,
    )
```
